32 devices in a mesh: fsdp: 4 (over y, x), seq: 8 (over z, core).
Axes of the slice: x: 2, y: 2, z: 4, core: 2. Of those that a mesh axis runs over, the one named last changes fastest.
Arguments:
- q_next: bfloat16 [4096, 4096], P(('fsdp', 'seq')), may hold values from -9 to 9
- k_next: bfloat16 [4096, 1024], P(('fsdp', 'seq')), may hold values from -4 to 4
- v_next: bfloat16 [4096, 1024], P(('fsdp', 'seq')), may hold values from -6 to 6
- seg_next: int32 [4, 1024], P('fsdp'), may hold values from 0 to 3, never falling along the last dimension, each value on 1 to 512 neighbouring positions
- q_prev: bfloat16 [4096, 4096], P(('fsdp', 'seq')), may hold values from -9 to 9
- k_prev: bfloat16 [4096, 1024], P(('fsdp', 'seq')), may hold values from -4 to 4
- v_prev: bfloat16 [4096, 1024], P(('fsdp', 'seq')), may hold values from -6 to 6
- seg_prev: int32 [4, 1024], P('fsdp'), may hold values from 0 to 3, never falling along the last dimension, each value on 1 to 512 neighbouring positions
- upstream: bfloat16 [4096, 4096], P(('fsdp', 'seq')), may hold values from -6 to 6
- flags: int32 [4, 1024], P('fsdp', 'seq'), may hold values from 0 to 1
Outputs:
- attn_next: bfloat16 [4096, 4096], P(('fsdp', 'seq'))
- grad_q: bfloat16 [4096, 4096], P(('fsdp', 'seq'))
- grad_k: bfloat16 [4096, 1024], P(('fsdp', 'seq'))
- grad_v: bfloat16 [4096, 1024], P(('fsdp', 'seq'))
The draws below stay inside these ranges and needn't reach their ends.
Inputs may be any that keep to these rules, and one draw needn't show every extreme that they name: `seg_next`: within each sequence the ids never fall and each id covers at most 512 consecutive positions; some id covers exactly 512. `seg_prev`: within each sequence the ids never fall and each id covers at most 512 consecutive positions; some id covers exactly 512.
All inputs are finite; a program needn't handle non-finite values.
Results may differ from the reference program's by a relative error of at most 0.0067.
Values may be sent and summed in bfloat16 or wider, within the bound.
A program may use at most 128 MiB of HBM per device.

```python
import math
import jax
import jax.numpy as jnp
import numpy as np
from jax import lax

HEADS = 32
KV_HEADS = 8
HEAD_DIM = 128
TOK_DEV = 128
BATCH = 4
SEQ = 1024
TOKENS = 4096
SEG_MOST = 512
BLOCK = 512


def draw_pair(key, marker):
    key = jax.random.fold_in(key, marker)
    query_key, keys_key = jax.random.split(key, 2)
    queries = jnp.clip(jax.random.normal(query_key, (TOKENS, HEADS * HEAD_DIM), jnp.float32), -4.0, 4.0)
    keys_all = jnp.clip(jax.random.normal(keys_key, (TOKENS, KV_HEADS * HEAD_DIM), jnp.float32), -4.0, 4.0)
    return (queries.astype(jnp.bfloat16), keys_all.astype(jnp.bfloat16))


def draw_q_next(key, part):
    return draw_pair(key, 11)[0]


def draw_k_next(key, part):
    return draw_pair(key, 11)[1]


def draw_q_prev(key, part):
    return draw_pair(key, 23)[0]


def draw_k_prev(key, part):
    return draw_pair(key, 23)[1]


def draw_flags(key, part):
    key = jax.random.fold_in(key, 37)
    level_key, dice_key = jax.random.split(key)
    levels = jax.random.randint(level_key, (BATCH, SEQ // TOK_DEV), 4, 11)
    limits = jnp.left_shift(jnp.ones_like(levels), levels)
    limit_rows = jnp.repeat(limits, TOK_DEV, axis=1)
    dice = jax.random.randint(dice_key, (BATCH, SEQ), 0, 1024)
    return (dice < limit_rows).astype(jnp.int32)


def block_scale(rng, extent, shards, low, top_value):
    def one(axis_at, blocks):
        draws = jax.random.uniform(jax.random.fold_in(jax.random.fold_in(rng, 6), axis_at), (blocks,), jnp.float32, low / len(shards), top_value / len(shards))
        return jnp.repeat(jnp.exp(draws), extent[axis_at] // blocks).reshape((-1,) + (1,) * (len(extent) - axis_at - 1))

    factor_of = one(*shards[0])
    for cut in shards[1:]:
        factor_of = factor_of * one(*cut)
    return factor_of


def length_profile(count, total, most, lean):
    portions = [(1 << 20) // math.isqrt(grade ** lean) + 1 for grade in range(2, count + 1)]
    surplus, given = total - most - (count - 1), [1] * (count - 1)
    while surplus > 0:
        candidates = [i for i in range(count - 1) if given[i] < most]
        whole, left = sum([portions[i] for i in candidates]), surplus
        for i in candidates:
            addition = min(most - given[i], max(1, left * portions[i] // whole), surplus)
            given[i] = given[i] + addition
            surplus = surplus - addition
    return np.array([most] + given)


def ragged_sizes(key, count, total, most, lean):
    if count == 2:
        one = jax.random.randint(key, (), max(1, total - most), min(most, total - 1) + 1)
        return jnp.stack([one, total - one])
    tallies = jnp.asarray(length_profile(count, total, most, lean), jnp.int32)
    pairs = (count - 1) // 2
    giver, taker = tallies[1:1 + 2 * pairs:2], tallies[2:2 + 2 * pairs:2]
    slack = jnp.minimum(giver - 1, most - taker)
    shifted = jax.random.randint(jax.random.fold_in(key, 1), (pairs,), 0, 1 << 20) % (slack + 1)
    tallies = tallies.at[1:1 + 2 * pairs:2].set(giver - shifted).at[2:2 + 2 * pairs:2].set(taker + shifted)
    return tallies[jax.random.permutation(jax.random.fold_in(key, 2), count)]


def noise(rng, extent, deviation, limit, pieces=(), kind=jnp.bfloat16):
    gain = block_scale(rng, extent, pieces, -0.22, 0.18) if pieces else 1.0
    entries = jax.random.normal(rng, extent, jnp.float32) * deviation * gain
    return jnp.minimum(jnp.maximum(entries, -limit), limit).astype(kind)


def setup_inputs(seed: int = 0) -> dict:
    arg_keys = jax.random.split(jax.random.key(seed), 11)
    q_next = draw_q_next(jax.random.fold_in(arg_keys[10], 71), 0)
    k_next = draw_k_next(jax.random.fold_in(arg_keys[10], 71), 0)
    v_next = noise(arg_keys[2], (TOKENS, KV_HEADS * HEAD_DIM), 1.0, 6.0, ((0, 32),))
    seg_next = jax.vmap(lambda own: jnp.searchsorted(jnp.cumsum(ragged_sizes(own, 2 * SEQ // SEG_MOST, SEQ, SEG_MOST, 1)), jnp.arange(SEQ), side="right"))(jax.random.split(arg_keys[3], BATCH)).reshape((BATCH, SEQ)).astype(jnp.int32)
    q_prev = draw_q_prev(jax.random.fold_in(arg_keys[10], 71), 0)
    k_prev = draw_k_prev(jax.random.fold_in(arg_keys[10], 71), 0)
    v_prev = noise(arg_keys[6], (TOKENS, KV_HEADS * HEAD_DIM), 1.0, 6.0, ((0, 32),))
    seg_prev = jax.vmap(lambda own: jnp.searchsorted(jnp.cumsum(ragged_sizes(own, 2 * SEQ // SEG_MOST, SEQ, SEG_MOST, 1)), jnp.arange(SEQ), side="right"))(jax.random.split(arg_keys[7], BATCH)).reshape((BATCH, SEQ)).astype(jnp.int32)
    upstream = noise(arg_keys[8], (TOKENS, HEADS * HEAD_DIM), 1.0, 6.0, ((0, 32),))
    flags = draw_flags(jax.random.fold_in(arg_keys[10], 71), 0)
    return dict(q_next=q_next, k_next=k_next, v_next=v_next, seg_next=seg_next, q_prev=q_prev, k_prev=k_prev, v_prev=v_prev, seg_prev=seg_prev, upstream=upstream, flags=flags)


def narrow(values):
    return lax.optimization_barrier(values.astype(jnp.bfloat16)).astype(jnp.float32)


def masked_probs(q_block, k_window, q_pos, k_pos, q_seg, k_seg):
    scale_factor = HEAD_DIM ** -0.5
    scores = jnp.einsum('qhd,khd->hqk', q_block.astype(jnp.float32), k_window.astype(jnp.float32)) * scale_factor
    keep_mask = (k_seg[None, :] == q_seg[:, None]) & (k_pos[None, :] <= q_pos[:, None])
    scores = jnp.where(keep_mask[None], scores, -1e30)
    row_max = jnp.max(scores, axis=-1, keepdims=True)
    expo_vals = jnp.exp(scores - row_max)
    return expo_vals / jnp.sum(expo_vals, axis=-1, keepdims=True)


def block_window(seq_ids, block_start):
    padded = jnp.concatenate([jnp.full((SEG_MOST,), -1, jnp.int32), seq_ids.astype(jnp.int32)])
    q_seg = lax.dynamic_slice_in_dim(seq_ids.astype(jnp.int32), block_start, BLOCK)
    k_seg = lax.dynamic_slice_in_dim(padded, block_start, SEG_MOST + BLOCK)
    q_pos = block_start + jnp.arange(BLOCK, dtype=jnp.int32)
    k_pos = block_start - SEG_MOST + jnp.arange(SEG_MOST + BLOCK, dtype=jnp.int32)
    return q_pos, k_pos, q_seg, k_seg


def pad_front(array):
    return jnp.concatenate([jnp.zeros((SEG_MOST,) + array.shape[1:], array.dtype), array], axis=0)


def forward_heads(q_heads, k_heads, v_heads, seq_ids):
    k_padded = pad_front(k_heads)
    v_padded = pad_front(v_heads)

    def block_step(block_idx, output):
        block_start = (block_idx * BLOCK).astype(jnp.int32)
        q_pos, k_pos, q_seg, k_seg = block_window(seq_ids, block_start)
        q_block = lax.dynamic_slice_in_dim(q_heads, block_start, BLOCK, 0)
        k_window = lax.dynamic_slice_in_dim(k_padded, block_start, SEG_MOST + BLOCK, 0)
        v_window = lax.dynamic_slice_in_dim(v_padded, block_start, SEG_MOST + BLOCK, 0)
        soft_probs = masked_probs(q_block, k_window, q_pos, k_pos, q_seg, k_seg)
        result = jnp.einsum('hqk,khd->qhd', narrow(soft_probs), v_window.astype(jnp.float32)).astype(jnp.bfloat16)
        return lax.dynamic_update_slice_in_dim(output, result, block_start, 0)

    return lax.fori_loop(0, SEQ // BLOCK, block_step, jnp.zeros(q_heads.shape, jnp.bfloat16))


def backward_heads(q_heads, k_heads, v_heads, d_heads, seq_ids):
    k_padded = pad_front(k_heads)
    v_padded = pad_front(v_heads)
    scale_factor = HEAD_DIM ** -0.5

    def block_step(block_idx, carry):
        grad_qh, k_grads, v_grads = carry
        block_start = (block_idx * BLOCK).astype(jnp.int32)
        q_pos, k_pos, q_seg, k_seg = block_window(seq_ids, block_start)
        q_block = lax.dynamic_slice_in_dim(q_heads, block_start, BLOCK, 0).astype(jnp.float32)
        d_block = lax.dynamic_slice_in_dim(d_heads, block_start, BLOCK, 0).astype(jnp.float32)
        k_window = lax.dynamic_slice_in_dim(k_padded, block_start, SEG_MOST + BLOCK, 0).astype(jnp.float32)
        v_window = lax.dynamic_slice_in_dim(v_padded, block_start, SEG_MOST + BLOCK, 0).astype(jnp.float32)
        soft_probs = masked_probs(q_block, k_window, q_pos, k_pos, q_seg, k_seg)
        d_probs = jnp.einsum('qhd,khd->hqk', d_block, v_window)
        row_delta = jnp.sum(soft_probs * d_probs, axis=-1, keepdims=True)
        d_scores = narrow(soft_probs * (d_probs - row_delta) * scale_factor)
        q_grad = jnp.einsum('hqk,khd->qhd', d_scores, k_window).astype(jnp.bfloat16)
        k_term = jnp.einsum('hqk,qhd->khd', d_scores, q_block)
        v_term = jnp.einsum('hqk,qhd->khd', narrow(soft_probs), d_block)
        grad_qh = lax.dynamic_update_slice_in_dim(grad_qh, q_grad, block_start, 0)
        k_old = lax.dynamic_slice_in_dim(k_grads, block_start, SEG_MOST + BLOCK, 0)
        v_old = lax.dynamic_slice_in_dim(v_grads, block_start, SEG_MOST + BLOCK, 0)
        k_grads = lax.dynamic_update_slice_in_dim(k_grads, k_old + k_term, block_start, 0)
        v_grads = lax.dynamic_update_slice_in_dim(v_grads, v_old + v_term, block_start, 0)
        return grad_qh, k_grads, v_grads

    buffer_shape = (SEG_MOST + SEQ,) + q_heads.shape[1:]
    start_carry = (jnp.zeros(q_heads.shape, jnp.bfloat16), jnp.zeros(buffer_shape, jnp.float32), jnp.zeros(buffer_shape, jnp.float32))
    grad_qh, k_grads, v_grads = lax.fori_loop(0, SEQ // BLOCK, block_step, start_carry)
    return grad_qh, k_grads[SEG_MOST:], v_grads[SEG_MOST:]


def reference(q_next, k_next, v_next, seg_next, q_prev, k_prev, v_prev, seg_prev, upstream, flags):
    group_size = HEADS // KV_HEADS

    def query_heads(array):
        return array.reshape(BATCH, SEQ, HEADS, HEAD_DIM)

    def shared_heads(array):
        return jnp.repeat(array.reshape(BATCH, SEQ, KV_HEADS, HEAD_DIM), group_size, axis=2)

    def group_sum(array):
        summed = jnp.sum(array.reshape(TOKENS, KV_HEADS, group_size, HEAD_DIM).astype(jnp.float32), axis=2)
        return summed.astype(jnp.bfloat16).reshape(TOKENS, KV_HEADS * HEAD_DIM)

    attn = lax.map(lambda members: forward_heads(*members), (query_heads(q_next), shared_heads(k_next), shared_heads(v_next), seg_next))
    attn_next = attn.reshape(TOKENS, HEADS * HEAD_DIM)
    flag_total = jnp.sum(flags.astype(jnp.float32))
    weight = flags.reshape(TOKENS, 1).astype(jnp.float32) * (TOKENS / jnp.maximum(flag_total, 1.0))
    cotangent = (upstream.astype(jnp.float32) * weight).astype(jnp.bfloat16)
    grads = lax.map(lambda members: backward_heads(*members), (query_heads(q_prev), shared_heads(k_prev), shared_heads(v_prev), query_heads(cotangent), seg_prev))
    grad_q = grads[0].reshape(TOKENS, HEADS * HEAD_DIM)
    grad_k = group_sum(grads[1])
    grad_v = group_sum(grads[2])
    return attn_next, grad_q, grad_k, grad_v
```

```python
import functools
import math

import jax
import jax.numpy as jnp
from jax import lax
from jax.experimental import pallas as pl
from jax.experimental.pallas import tpu as pltpu
from jax.sharding import PartitionSpec as P

HEAD_DIM = 128
SEG_MOST = 512
NT = (((1,), (1,)), ((), ()))


def dot_nt(a, b):
    return lax.dot_general(a, b, NT, preferred_element_type=jnp.float32)


def dot_nn(a, b):
    return jnp.dot(a, b, preferred_element_type=jnp.float32)


def stack_heads(array):
    group = array.shape[1] // HEAD_DIM
    return jnp.concatenate(
        [array[:, g * HEAD_DIM : (g + 1) * HEAD_DIM] for g in range(group)], axis=0
    )


def weights_t(k_win, q_all, bias, group):
    factor = HEAD_DIM ** (-0.5) * math.log2(math.e)
    scores = dot_nt(k_win, q_all) * factor + jnp.concatenate([bias] * group, axis=1)
    top = jnp.max(scores, axis=0, keepdims=True)
    expo = jnp.exp2(scores - top)
    return expo, jnp.sum(expo, axis=0, keepdims=True)


def forward_kernel(blocks, bias_ref, q_ref, *refs):
    k_refs, v_refs, out_ref = refs[:blocks], refs[blocks : 2 * blocks], refs[2 * blocks]
    rows = q_ref.shape[0]
    group = q_ref.shape[1] // HEAD_DIM
    k_win = jnp.concatenate([r[...] for r in k_refs], axis=0)
    v_win = jnp.concatenate([r[...] for r in v_refs], axis=0)
    q_all = stack_heads(q_ref[...])
    expo, total = weights_t(k_win, q_all, bias_ref[...], group)
    out_t = dot_nn(v_win.T, expo.astype(jnp.bfloat16)) * (1.0 / total)
    for g in range(group):
        out_ref[:, g * HEAD_DIM : (g + 1) * HEAD_DIM] = (
            out_t[:, g * rows : (g + 1) * rows].T.astype(out_ref.dtype)
        )


def backward_kernel(blocks, bias_ref, weight_ref, q_ref, up_ref, *refs):
    k_refs, v_refs = refs[:blocks], refs[blocks : 2 * blocks]
    dq_ref = refs[2 * blocks]
    dk_refs = refs[2 * blocks + 1 : 3 * blocks + 1]
    dv_refs = refs[3 * blocks + 1 :]
    rows = q_ref.shape[0]
    group = q_ref.shape[1] // HEAD_DIM
    k_win = jnp.concatenate([r[...] for r in k_refs], axis=0)
    v_win = jnp.concatenate([r[...] for r in v_refs], axis=0)
    q_all = stack_heads(q_ref[...])
    cot = (up_ref[...].astype(jnp.float32) * weight_ref[...]).astype(jnp.bfloat16)
    d_all = stack_heads(cot)
    expo, total = weights_t(k_win, q_all, bias_ref[...], group)
    probs = expo * (1.0 / total)
    d_probs = dot_nt(v_win, d_all)
    delta = jnp.sum(probs * d_probs, axis=0, keepdims=True)
    d_scores = (probs * (d_probs - delta) * (HEAD_DIM ** (-0.5))).astype(jnp.bfloat16)
    dv = dot_nn(probs.astype(jnp.bfloat16), d_all)
    dk = dot_nn(d_scores, q_all)
    for b in range(blocks):
        dk_refs[b][...] = dk[b * rows : (b + 1) * rows].astype(dk_refs[b].dtype)
        dv_refs[b][...] = dv[b * rows : (b + 1) * rows].astype(dv_refs[b].dtype)
    dq_t = dot_nn(k_win.T, d_scores)
    for g in range(group):
        dq_ref[:, g * HEAD_DIM : (g + 1) * HEAD_DIM] = (
            dq_t[:, g * rows : (g + 1) * rows].T.astype(dq_ref.dtype)
        )


def attend(kernel, name, bias, columns, wide, k_blocks, v_blocks, grads, dots):
    blocks = len(k_blocks)
    rows, width = k_blocks[0].shape
    kv_heads = width // HEAD_DIM
    group_width = wide[0].shape[1] // kv_heads

    def whole(array):
        return pl.BlockSpec(array.shape, lambda j: (0, 0))

    narrow_spec = pl.BlockSpec((rows, HEAD_DIM), lambda j: (0, j))
    wide_spec = pl.BlockSpec((rows, group_width), lambda j: (0, j))
    wide_shape = jax.ShapeDtypeStruct(wide[0].shape, jnp.bfloat16)
    narrow_shape = jax.ShapeDtypeStruct((rows, width), jnp.bfloat16)
    flops = dots * 2 * rows * wide[0].shape[1] * blocks * rows
    moved = 2 * rows * ((len(wide) + 1) * wide[0].shape[1] + (2 + grads) * blocks * width)
    return pl.pallas_call(
        functools.partial(kernel, blocks),
        grid=(kv_heads,),
        in_specs=[whole(bias)]
        + [whole(c) for c in columns]
        + [wide_spec] * len(wide)
        + [narrow_spec] * (2 * blocks),
        out_specs=[wide_spec] + [narrow_spec] * (grads * blocks),
        out_shape=[wide_shape] + [narrow_shape] * (grads * blocks),
        compiler_params=pltpu.CompilerParams(
            dimension_semantics=("arbitrary",), vmem_limit_bytes=48 * 1024 * 1024
        ),
        cost_estimate=pl.CostEstimate(
            flops=2 * flops,
            bytes_accessed=moved,
            transcendentals=rows * wide[0].shape[1] * blocks,
        ),
        name=name,
    )(bias, *columns, *wide, *k_blocks, *v_blocks)


def shifted(arrays, distance):
    size = lax.axis_size("seq")
    route = [(i, i + distance) for i in range(size) if 0 <= i + distance < size]
    return [lax.ppermute(a, "seq", route) for a in arrays]


def swapped(arrays):
    size = lax.axis_size("seq")
    route = [(i, i ^ 1) for i in range(size) if (i ^ 1) < size]
    return [lax.ppermute(a, "seq", route) for a in arrays]


def pick(pred, one, other):
    return [jnp.where(pred, a, b) for a, b in zip(one, other)]


def after(arrays, others):
    held = lax.optimization_barrier((tuple(arrays), tuple(others)))
    return list(held[0])


def gather_window(local, hops, is_even):
    got = {0: local}
    for h in range(2, hops + 2, 2):
        got[h] = shifted(got[h - 2], 2)
    for h in range(1, hops + 1, 2):
        got[h] = swapped(pick(is_even, got[h - 1], got[h + 1]))
    return got


def return_sums(parts, hops, is_even):
    came = {h: swapped(parts[h]) for h in range(1, hops + 1, 2)}
    top = hops + hops % 2

    def joined(h):
        terms = [p.astype(jnp.float32) for p in parts[h]] if h in parts else None
        low = came.get(h - 1)
        high = came.get(h + 1)
        if low is None:
            extra = [jnp.where(is_even, b, jnp.zeros_like(b)) for b in high]
        elif high is None:
            extra = [jnp.where(is_even, jnp.zeros_like(a), a) for a in low]
        else:
            extra = pick(is_even, high, low)
        if terms is None:
            return [e.astype(jnp.float32) for e in extra]
        return [t + e.astype(jnp.float32) for t, e in zip(terms, extra)]

    running = joined(top)
    for h in range(top - 2, -1, -2):
        back = shifted([r.astype(jnp.bfloat16) for r in running], -2)
        running = [t + b.astype(jnp.float32) for t, b in zip(joined(h), back)]
    return [r.astype(jnp.bfloat16) for r in running]


def total_over(value, axes):
    for axis in axes:
        size = lax.axis_size(axis)
        if size & (size - 1):
            value = lax.psum(value, axis)
            continue
        step = 1
        while step < size:
            value = value + lax.ppermute(value, axis, [(i, i ^ step) for i in range(size)])
            step *= 2
    return value


def window_bias(seq_ids, rows, hops):
    first = lax.axis_index("seq") * rows
    width = (hops + 1) * rows
    padded = jnp.concatenate([jnp.full((hops * rows,), -1, jnp.int32), seq_ids])
    k_seg = lax.dynamic_slice_in_dim(padded, first, width)
    q_seg = lax.dynamic_slice_in_dim(seq_ids, first, rows)
    k_pos = lax.broadcasted_iota(jnp.int32, (width, rows), 0) - hops * rows
    q_pos = lax.broadcasted_iota(jnp.int32, (width, rows), 1)
    keep = (k_seg[:, None] == q_seg[None, :]) & (k_pos <= q_pos)
    return jnp.where(keep, 0.0, -1e30).astype(jnp.float32)


def body(q_next, k_next, v_next, seg_next, q_prev, k_prev, v_prev, seg_prev, upstream, flags):
    rows = q_next.shape[0]
    seq_size = lax.axis_size("seq")
    token_total = rows * lax.axis_size("fsdp") * seq_size
    hops = min((min(SEG_MOST, rows * seq_size) - 2) // rows + 1, seq_size - 1)
    is_even = lax.axis_index("seq") % 2 == 0
    order = range(hops, -1, -1)

    prev = gather_window([k_prev, v_prev], hops, is_even)
    last = hops + hops % 2
    local_next = after([k_next, v_next], prev[last])
    nxt = gather_window(local_next, hops, is_even)

    flag_total = total_over(jnp.sum(flags.astype(jnp.float32)).reshape(1, 1), ("seq", "fsdp"))
    weight = flags.reshape(rows, 1).astype(jnp.float32) * (
        token_total / jnp.maximum(flag_total, 1.0)
    )
    results = attend(
        backward_kernel,
        "backward",
        window_bias(seg_prev[0], rows, hops),
        [weight],
        [q_prev, upstream],
        [prev[h][0] for h in order],
        [prev[h][1] for h in order],
        2,
        5,
    )
    grad_q = results[0]
    blocks = hops + 1
    parts = {
        h: [results[1 + blocks - 1 - h], results[1 + 2 * blocks - 1 - h]]
        for h in range(blocks)
    }
    grad_k, grad_v = return_sums(parts, hops, is_even)
    (attn_next,) = attend(
        forward_kernel,
        "forward",
        window_bias(seg_next[0], rows, hops),
        [],
        [q_next],
        [nxt[h][0] for h in order],
        [nxt[h][1] for h in order],
        0,
        2,
    )
    return (attn_next, grad_q, grad_k, grad_v)


def solution(mesh):
    tokens = P(("fsdp", "seq"), None)
    ids = P("fsdp", None)
    return jax.shard_map(
        body,
        mesh=mesh,
        in_specs=(
            tokens,
            tokens,
            tokens,
            ids,
            tokens,
            tokens,
            tokens,
            ids,
            tokens,
            P("fsdp", "seq"),
        ),
        out_specs=(tokens, tokens, tokens, tokens),
        check_vma=False,
    )
```

```python
import functools
import math

import jax
import jax.numpy as jnp
from jax import lax
from jax.experimental import pallas as pl
from jax.experimental.pallas import tpu as pltpu
from jax.sharding import PartitionSpec as P

HEAD_DIM = 128
SEG_MOST = 512
NT = (((1,), (1,)), ((), ()))
MESH = pl.DeviceIdType.MESH


def dot_nt(a, b):
    return lax.dot_general(a, b, NT, preferred_element_type=jnp.float32)


def dot_nn(a, b):
    return jnp.dot(a, b, preferred_element_type=jnp.float32)


def stack_heads(array):
    group = array.shape[1] // HEAD_DIM
    return jnp.concatenate(
        [array[:, g * HEAD_DIM : (g + 1) * HEAD_DIM] for g in range(group)], axis=0
    )


def weights_t(k_win, q_all, bias, group):
    factor = HEAD_DIM ** (-0.5) * math.log2(math.e)
    scores = dot_nt(k_win, q_all) * factor + jnp.concatenate([bias] * group, axis=1)
    top = jnp.max(scores, axis=0, keepdims=True)
    expo = jnp.exp2(scores - top)
    return expo, jnp.sum(expo, axis=0, keepdims=True)


def down_rows(row, rows):
    return jnp.broadcast_to(row.astype(jnp.float32), (rows, rows)).T


def kernel(
    hops,
    sizes,
    q_next,
    k_next,
    v_next,
    seg_next,
    q_prev,
    k_prev,
    v_prev,
    seg_prev,
    upstream,
    flags,
    attn_out,
    dq_out,
    dk_out,
    dv_out,
    window,
    bias,
    weight,
    grads,
    grad_in,
    sums,
    sums_in,
    count,
    count_in,
    local_sem,
    send_sem,
    recv_sem,
    grad_send,
    grad_recv,
    count_send,
    count_recv,
):
    fsdp_size, seq_size = sizes
    rows = q_next.shape[0]
    kv_heads = k_next.shape[1] // HEAD_DIM
    wide = q_next.shape[1] // kv_heads
    group = wide // HEAD_DIM
    top = hops + hops % 2
    me = lax.axis_index("seq")
    row_of = lax.axis_index("fsdp")
    parity = lax.rem(me, 2)
    partner = me + 1 - 2 * parity
    has_after = me + 2 < seq_size
    has_before = me >= 2

    def flipped(value, step):
        return value + step - 2 * step * lax.rem(value // step, 2)

    count_to = []
    greet = []
    for axis, size in (("fsdp", fsdp_size), ("seq", seq_size)):
        step = 1
        while step < size:
            if axis == "seq":
                count_to.append((row_of, flipped(me, step)))
            else:
                count_to.append((flipped(row_of, step), me))
            if (axis, step) != ("seq", 2):
                greet.append(count_to[-1])
            step *= 2

    barrier = pltpu.get_barrier_semaphore()

    @pl.when(has_after)
    def _():
        pl.semaphore_signal(barrier, inc=1, device_id=(row_of, me + 2), device_id_type=MESH)

    @pl.when(has_before)
    def _():
        pl.semaphore_signal(barrier, inc=1, device_id=(row_of, me - 2), device_id_type=MESH)

    for target in greet:
        pl.semaphore_signal(barrier, inc=1, device_id=target, device_id_type=MESH)

    def own(m, part, j):
        source = ((k_prev, v_prev), (k_next, v_next))[m][part]
        return pltpu.make_async_copy(
            source.at[:, pl.ds(pl.multiple_of(j * HEAD_DIM, HEAD_DIM), HEAD_DIM)],
            window.at[m, 0, j, pl.ds(part * rows, rows)],
            local_sem.at[m, part, j],
        )

    for m in range(2):

        @pl.loop(0, kv_heads)
        def _(j, m=m):
            own(m, 0, j).start()
            own(m, 1, j).start()

    neighbours = jnp.where(has_after, 1, 0) + jnp.where(has_before, 1, 0)
    pl.semaphore_wait(barrier, len(greet) + neighbours)

    def hop(m, o, j):
        return pltpu.make_async_remote_copy(
            src_ref=window.at[m, o - 2, j],
            dst_ref=window.at[m, o, j],
            send_sem=send_sem.at[m, o, j],
            recv_sem=recv_sem.at[m, o, j],
            device_id=(row_of, me + 2),
            device_id_type=MESH,
        )

    def swap(m, o, j):
        return pltpu.make_async_remote_copy(
            src_ref=window.at[m, o - 1 + 2 * parity, j],
            dst_ref=window.at[m, o, j],
            send_sem=send_sem.at[m, o, j],
            recv_sem=recv_sem.at[m, o, j],
            device_id=(row_of, partner),
            device_id_type=MESH,
        )

    def swap_start(m, o, j, by):
        @pl.when((parity == by) & (partner >= o))
        def _():
            swap(m, o, j).start()

    def start_hop(m, o, j):
        @pl.when(has_after & (me >= o - 2))
        def _():
            hop(m, o, j).start()

    def arrive_hop(m, o, j):
        @pl.when(me >= o)
        def _():
            hop(m, o, j).wait_recv()

    def arrive_swap(m, o, j):
        @pl.when(me >= o)
        def _():
            swap(m, o, j).wait_recv()

    def first_hops(m):
        @pl.loop(0, kv_heads)
        def _(j):
            own(m, 0, j).wait()
            own(m, 1, j).wait()
            start_hop(m, 2, j)

    def on_hop(m, o, j):
        arrive_hop(m, o, j)
        if o + 2 <= top:
            start_hop(m, o + 2, j)
        if o - 1 <= hops:
            if o == 2:
                swap_start(m, 1, j, 0)
            swap_start(m, o - 1, j, 1)
        if o + 1 <= hops:
            swap_start(m, o + 1, j, 0)

    first_hops(0)

    here = jnp.sum(flags[...].astype(jnp.float32), axis=1, keepdims=True)
    count[0] = jnp.broadcast_to(here, count.shape[1:])
    for s, target in enumerate(count_to):
        copy = pltpu.make_async_remote_copy(
            src_ref=count.at[s],
            dst_ref=count_in.at[s],
            send_sem=count_send.at[s],
            recv_sem=count_recv.at[s],
            device_id=target,
            device_id_type=MESH,
        )
        copy.start()
        if s == 0:
            for o in range(1, top + 1):

                @pl.when(me < o)
                def _(o=o):
                    for m in range(2):

                        @pl.loop(0, kv_heads)
                        def _(j):
                            window[m, o, j] = jnp.zeros(window.shape[3:], window.dtype)

            @pl.when(jnp.logical_not(has_after))
            def _():
                for part in range(top // 2):

                    @pl.loop(0, kv_heads)
                    def _(j):
                        sums_in[part, j] = jnp.zeros(sums_in.shape[2:], sums_in.dtype)

            for m, seg in ((0, seg_prev), (1, seg_next)):
                q_seg = seg[:, pl.ds(pl.multiple_of(me * rows, rows), rows)].astype(jnp.float32)
                k_at = lax.broadcasted_iota(jnp.int32, (rows, rows), 0)
                q_at = lax.broadcasted_iota(jnp.int32, (rows, rows), 1)
                for o in range(hops + 1):
                    block = jnp.maximum(me - o, 0)
                    k_seg = seg[:, pl.ds(pl.multiple_of(block * rows, rows), rows)]
                    keep = (down_rows(k_seg, rows) == q_seg) & (k_at - o * rows <= q_at)
                    gone = jnp.where(me >= o, 0.0, -1e30)
                    bias[m, pl.ds(o * rows, rows)] = jnp.where(keep, gone, -1e30)
        copy.wait()
        count[s + 1] = count[s] + count_in[s]
    token_total = float(rows * fsdp_size * seq_size)
    scale = token_total / jnp.maximum(count[len(count_to)][:1], 1.0)
    weight[...] = down_rows(flags[...], rows) * scale[:, :1]

    @pl.loop(0, kv_heads)
    def _(j):
        on_hop(0, 2, j)

    first_hops(1)

    def blocks_of(m, part, j):
        return jnp.concatenate(
            [window[m, o, j, part * rows : (part + 1) * rows] for o in range(hops + 1)], axis=0
        )

    def columns(j):
        return pl.ds(pl.multiple_of(j * wide, wide), wide)

    def backward(j):
        k_win = blocks_of(0, 0, j)
        v_win = blocks_of(0, 1, j)
        q_all = stack_heads(q_prev[:, columns(j)])
        up_all = stack_heads(upstream[:, columns(j)]).astype(jnp.float32)
        d_all = (up_all * jnp.concatenate([weight[...]] * group, axis=0)).astype(jnp.bfloat16)
        expo, total = weights_t(k_win, q_all, bias[0], group)
        probs = expo * (1.0 / total)
        d_probs = dot_nt(v_win, d_all)
        delta = jnp.sum(probs * d_probs, axis=0, keepdims=True)
        d_scores = (probs * (d_probs - delta) * (HEAD_DIM ** (-0.5))).astype(jnp.bfloat16)
        dv = dot_nn(probs.astype(jnp.bfloat16), d_all).astype(jnp.bfloat16)
        dk = dot_nn(d_scores, q_all).astype(jnp.bfloat16)
        for o in range(hops + 1):
            grads[o, j, :rows] = dk[o * rows : (o + 1) * rows]
            grads[o, j, rows:] = dv[o * rows : (o + 1) * rows]
        dq_t = dot_nn(k_win.T, d_scores)
        dq_out[:, columns(j)] = jnp.concatenate(
            [dq_t[:, g * rows : (g + 1) * rows].T for g in range(group)], axis=1
        ).astype(dq_out.dtype)

    def forward(j):
        k_win = blocks_of(1, 0, j)
        v_win = blocks_of(1, 1, j)
        q_all = stack_heads(q_next[:, columns(j)])
        expo, total = weights_t(k_win, q_all, bias[1], group)
        out_t = dot_nn(v_win.T, expo.astype(jnp.bfloat16)) * (1.0 / total)
        attn_out[:, columns(j)] = jnp.concatenate(
            [out_t[:, g * rows : (g + 1) * rows].T for g in range(group)], axis=1
        ).astype(attn_out.dtype)

    def later_hops(m, j):
        for o in range(4, top + 1, 2):
            on_hop(m, o, j)

    def grad_swap(o, j):
        return pltpu.make_async_remote_copy(
            src_ref=grads.at[o, j],
            dst_ref=grad_in.at[o // 2, j],
            send_sem=grad_send.at[o, j],
            recv_sem=grad_recv.at[o, j],
            device_id=(row_of, partner),
            device_id_type=MESH,
        )

    def sum_back(o, j):
        return pltpu.make_async_remote_copy(
            src_ref=sums.at[o // 2 - 1, j],
            dst_ref=sums_in.at[o // 2 - 1, j],
            send_sem=grad_send.at[o, j],
            recv_sem=grad_recv.at[o, j],
            device_id=(row_of, me - 2),
            device_id_type=MESH,
        )

    def joined(o, j):
        even = jnp.where(parity == 0, 1.0, 0.0)
        acc = jnp.zeros(grads.shape[2:], jnp.float32)
        if o <= hops:
            acc = grads[o, j].astype(jnp.float32)
        if o + 1 <= hops:
            acc = acc + grad_in[o // 2, j].astype(jnp.float32) * even
        if o > 0:
            acc = acc + grad_in[o // 2 - 1, j].astype(jnp.float32) * (1.0 - even)
        if o + 2 <= top:
            acc = acc + sums_in[o // 2, j].astype(jnp.float32)
        return acc

    def send_sum(o, j):
        sums[o // 2 - 1, j] = joined(o, j).astype(sums.dtype)

        @pl.when(has_before)
        def _():
            sum_back(o, j).start()

    def arrive_sum(o, j):
        @pl.when(has_after)
        def _():
            sum_back(o, j).wait_recv()

    def first_sum(j):
        for o in range(1, hops + 1, 2):
            grad_swap(o, j).wait_recv()
        send_sum(top, j)

    def ready(m, j):
        for o in range(1, hops + 1, 2):
            arrive_swap(m, o, j)

    later_hops(0, 0)

    @pl.loop(0, kv_heads)
    def _(j):
        @pl.when(j + 1 < kv_heads)
        def _():
            later_hops(0, j + 1)

        ready(0, j)
        backward(j)
        for o in range(1, hops + 1, 2):
            grad_swap(o, j).start()

        @pl.when(j > 0)
        def _():
            first_sum(j - 1)

    first_sum(kv_heads - 1)

    @pl.loop(0, kv_heads)
    def _(j):
        on_hop(1, 2, j)
        for o in range(top - 2, 0, -2):
            arrive_sum(o + 2, j)
            send_sum(o, j)

    later_hops(1, 0)

    @pl.loop(0, kv_heads)
    def _(j):
        @pl.when(j + 1 < kv_heads)
        def _():
            later_hops(1, j + 1)

        ready(1, j)
        forward(j)

    @pl.loop(0, kv_heads)
    def _(j):
        arrive_sum(2, j)
        acc = joined(0, j).astype(jnp.bfloat16)
        spot = pl.ds(pl.multiple_of(j * HEAD_DIM, HEAD_DIM), HEAD_DIM)
        dk_out[:, spot] = acc[:rows]
        dv_out[:, spot] = acc[rows:]

    @pl.loop(0, kv_heads)
    def _(j):
        for m in range(2):
            for o in range(2, top + 1, 2):

                @pl.when(has_after & (me >= o - 2))
                def _(m=m, o=o):
                    hop(m, o, j).wait_send()

            for o in range(1, hops + 1, 2):

                @pl.when(partner >= o)
                def _(m=m, o=o):
                    swap(m, o, j).wait_send()

        for o in range(1, hops + 1, 2):
            grad_swap(o, j).wait_send()
        for o in range(2, top + 1, 2):

            @pl.when(has_before)
            def _(o=o):
                sum_back(o, j).wait_send()


def make_body(fsdp_size, seq_size):
    def body(q_next, k_next, v_next, seg_next, q_prev, k_prev, v_prev, seg_prev, upstream, flags):
        rows, width = k_next.shape
        kv_heads = width // HEAD_DIM
        hops = min((min(SEG_MOST, rows * seq_size) - 2) // rows + 1, seq_size - 1)
        top = hops + hops % 2
        steps = fsdp_size.bit_length() + seq_size.bit_length() - 2
        piece = (2 * rows, HEAD_DIM)
        near = pl.BlockSpec(memory_space=pltpu.VMEM)
        far = pl.BlockSpec(memory_space=pl.ANY)
        call = pl.pallas_call(
            functools.partial(kernel, hops, (fsdp_size, seq_size)),
            in_specs=[near, far, far, near, near, far, far, near, near, near],
            out_specs=[near] * 4,
            out_shape=[
                jax.ShapeDtypeStruct(q_next.shape, jnp.bfloat16),
                jax.ShapeDtypeStruct(q_prev.shape, jnp.bfloat16),
                jax.ShapeDtypeStruct(k_prev.shape, jnp.bfloat16),
                jax.ShapeDtypeStruct(v_prev.shape, jnp.bfloat16),
            ],
            scratch_shapes=[
                pltpu.VMEM((2, top + 1, kv_heads) + piece, jnp.bfloat16),
                pltpu.VMEM((2, (hops + 1) * rows, rows), jnp.float32),
                pltpu.VMEM((rows, rows), jnp.float32),
                pltpu.VMEM((hops + 1, kv_heads) + piece, jnp.bfloat16),
                pltpu.VMEM(((hops + 1) // 2, kv_heads) + piece, jnp.bfloat16),
                pltpu.VMEM((top // 2, kv_heads) + piece, jnp.bfloat16),
                pltpu.VMEM((top // 2, kv_heads) + piece, jnp.bfloat16),
                pltpu.VMEM((steps + 1, 8, 128), jnp.float32),
                pltpu.VMEM((steps, 8, 128), jnp.float32),
                pltpu.SemaphoreType.DMA((2, 2, kv_heads)),
                pltpu.SemaphoreType.DMA((2, top + 1, kv_heads)),
                pltpu.SemaphoreType.DMA((2, top + 1, kv_heads)),
                pltpu.SemaphoreType.DMA((top + 1, kv_heads)),
                pltpu.SemaphoreType.DMA((top + 1, kv_heads)),
                pltpu.SemaphoreType.DMA((steps,)),
                pltpu.SemaphoreType.DMA((steps,)),
            ],
            compiler_params=pltpu.CompilerParams(
                collective_id=0, has_side_effects=True, vmem_limit_bytes=60 * 1024 * 1024
            ),
            name="attention_pair",
        )
        return tuple(
            call(
                q_next,
                k_next,
                v_next,
                seg_next,
                q_prev,
                k_prev,
                v_prev,
                seg_prev,
                upstream,
                flags,
            )
        )

    return body


def solution(mesh):
    tokens = P(("fsdp", "seq"), None)
    ids = P("fsdp", None)
    return jax.shard_map(
        make_body(mesh.shape["fsdp"], mesh.shape["seq"]),
        mesh=mesh,
        in_specs=(
            tokens,
            tokens,
            tokens,
            ids,
            tokens,
            tokens,
            tokens,
            ids,
            tokens,
            P("fsdp", "seq"),
        ),
        out_specs=(tokens, tokens, tokens, tokens),
        check_vma=False,
    )
```

```python
import functools
import math

import jax
import jax.numpy as jnp
from jax import lax
from jax.experimental import pallas as pl
from jax.experimental.pallas import tpu as pltpu
from jax.sharding import PartitionSpec as P

HEAD_DIM = 128
SEG_MOST = 512
NT = (((1,), (1,)), ((), ()))
MESH = pl.DeviceIdType.MESH


def dot_nt(a, b):
    return lax.dot_general(a, b, NT, preferred_element_type=jnp.float32)


def dot_nn(a, b):
    return jnp.dot(a, b, preferred_element_type=jnp.float32)


def stack_heads(array):
    group = array.shape[1] // HEAD_DIM
    return jnp.concatenate(
        [array[:, g * HEAD_DIM : (g + 1) * HEAD_DIM] for g in range(group)], axis=0
    )


def weights_t(k_win, q_all, bias, group):
    factor = HEAD_DIM ** (-0.5) * math.log2(math.e)
    scores = dot_nt(k_win, q_all) * factor + jnp.concatenate([bias] * group, axis=1)
    top = jnp.max(scores, axis=0, keepdims=True)
    expo = jnp.exp2(scores - top)
    return expo, jnp.sum(expo, axis=0, keepdims=True)


def down_rows(row, rows):
    return jnp.broadcast_to(row.astype(jnp.float32), (rows, rows)).T


def kernel(
    hops,
    sizes,
    q_next_far,
    k_next,
    v_next,
    seg_next,
    q_prev_far,
    k_prev,
    v_prev,
    seg_prev,
    upstream_far,
    flags,
    attn_out,
    dq_out,
    dk_out,
    dv_out,
    q_next,
    q_prev,
    upstream,
    wide_sem,
    window,
    bias,
    weight,
    grads,
    grad_in,
    sums,
    sums_in,
    count,
    count_in,
    local_sem,
    send_sem,
    recv_sem,
    grad_send,
    grad_recv,
    count_send,
    count_recv,
):
    fsdp_size, seq_size = sizes
    rows = q_next.shape[0]
    kv_heads = k_next.shape[1] // HEAD_DIM
    wide = q_next.shape[1] // kv_heads
    group = wide // HEAD_DIM
    top = hops + hops % 2
    me = lax.axis_index("seq")
    row_of = lax.axis_index("fsdp")
    parity = lax.rem(me, 2)
    partner = me + 1 - 2 * parity
    has_after = me + 2 < seq_size
    has_before = me >= 2

    def flipped(value, step):
        return value + step - 2 * step * lax.rem(value // step, 2)

    count_to = []
    greet = []
    for axis, low, size in (("seq", 2, seq_size), ("seq", 1, 2), ("fsdp", 1, fsdp_size)):
        step = low
        while step < size:
            if axis == "seq":
                count_to.append((row_of, flipped(me, step)))
            else:
                count_to.append((flipped(row_of, step), me))
            if (axis, step) != ("seq", 2):
                greet.append(count_to[-1])
            step *= 2

    barrier = pltpu.get_barrier_semaphore()

    @pl.when(has_after)
    def _():
        pl.semaphore_signal(barrier, inc=1, device_id=(row_of, me + 2), device_id_type=MESH)

    @pl.when(has_before)
    def _():
        pl.semaphore_signal(barrier, inc=1, device_id=(row_of, me - 2), device_id_type=MESH)

    for target in greet:
        pl.semaphore_signal(barrier, inc=1, device_id=target, device_id_type=MESH)

    def own(m, part, j):
        source = ((k_prev, v_prev), (k_next, v_next))[m][part]
        return pltpu.make_async_copy(
            source.at[:, pl.ds(pl.multiple_of(j * HEAD_DIM, HEAD_DIM), HEAD_DIM)],
            window.at[m, 0, j, pl.ds(part * rows, rows)],
            local_sem.at[m, part, j],
        )

    for m in range(2):

        @pl.loop(0, kv_heads)
        def _(j, m=m):
            own(m, 0, j).start()
            own(m, 1, j).start()

    wide_copies = [
        pltpu.make_async_copy(source, target, wide_sem.at[i])
        for i, (source, target) in enumerate(
            ((q_prev_far, q_prev), (upstream_far, upstream), (q_next_far, q_next))
        )
    ]
    for copy in wide_copies:
        copy.start()

    neighbours = jnp.where(has_after, 1, 0) + jnp.where(has_before, 1, 0)
    pl.semaphore_wait(barrier, len(greet) + neighbours)

    def hop(m, o, j):
        return pltpu.make_async_remote_copy(
            src_ref=window.at[m, o - 2, j],
            dst_ref=window.at[m, o, j],
            send_sem=send_sem.at[m, o, j],
            recv_sem=recv_sem.at[m, o, j],
            device_id=(row_of, me + 2),
            device_id_type=MESH,
        )

    def swap(m, o, j):
        return pltpu.make_async_remote_copy(
            src_ref=window.at[m, o - 1 + 2 * parity, j],
            dst_ref=window.at[m, o, j],
            send_sem=send_sem.at[m, o, j],
            recv_sem=recv_sem.at[m, o, j],
            device_id=(row_of, partner),
            device_id_type=MESH,
        )

    def swap_start(m, o, j, by):
        @pl.when((parity == by) & (partner >= o))
        def _():
            swap(m, o, j).start()

    def start_hop(m, o, j):
        @pl.when(has_after & (me >= o - 2))
        def _():
            hop(m, o, j).start()

    def arrive_hop(m, o, j):
        @pl.when(me >= o)
        def _():
            hop(m, o, j).wait_recv()

    def arrive_swap(m, o, j):
        @pl.when(me >= o)
        def _():
            swap(m, o, j).wait_recv()

    def first_hops(m, low=0, high=kv_heads):
        @pl.loop(low, high)
        def _(j):
            own(m, 0, j).wait()
            own(m, 1, j).wait()
            start_hop(m, 2, j)

    def on_hop(m, o, j):
        arrive_hop(m, o, j)
        if o + 2 <= top:
            start_hop(m, o + 2, j)
        if o - 1 <= hops:
            if o == 2:
                swap_start(m, 1, j, 0)
            swap_start(m, o - 1, j, 1)
        if o + 1 <= hops:
            swap_start(m, o + 1, j, 0)

    here = jnp.sum(flags[...].astype(jnp.float32), axis=1, keepdims=True)
    count[0] = jnp.broadcast_to(here, count.shape[1:])
    chunk = -(-kv_heads // len(count_to))
    for s, target in enumerate(count_to):
        copy = pltpu.make_async_remote_copy(
            src_ref=count.at[s],
            dst_ref=count_in.at[s],
            send_sem=count_send.at[s],
            recv_sem=count_recv.at[s],
            device_id=target,
            device_id_type=MESH,
        )
        copy.start()
        if s * chunk < kv_heads:
            first_hops(0, s * chunk, min((s + 1) * chunk, kv_heads))
        if s == 0:
            for o in range(1, top + 1):

                @pl.when(me < o)
                def _(o=o):
                    for m in range(2):

                        @pl.loop(0, kv_heads)
                        def _(j):
                            window[m, o, j] = jnp.zeros(window.shape[3:], window.dtype)

            @pl.when(jnp.logical_not(has_after))
            def _():
                for part in range(top // 2):

                    @pl.loop(0, kv_heads)
                    def _(j):
                        sums_in[part, j] = jnp.zeros(sums_in.shape[2:], sums_in.dtype)

            for m, seg in ((0, seg_prev), (1, seg_next)):
                q_seg = seg[:, pl.ds(pl.multiple_of(me * rows, rows), rows)].astype(jnp.float32)
                k_at = lax.broadcasted_iota(jnp.int32, (rows, rows), 0)
                q_at = lax.broadcasted_iota(jnp.int32, (rows, rows), 1)
                for o in range(hops + 1):
                    block = jnp.maximum(me - o, 0)
                    k_seg = seg[:, pl.ds(pl.multiple_of(block * rows, rows), rows)]
                    keep = (down_rows(k_seg, rows) == q_seg) & (k_at - o * rows <= q_at)
                    gone = jnp.where(me >= o, 0.0, -1e30)
                    bias[m, pl.ds(o * rows, rows)] = jnp.where(keep, gone, -1e30)
        copy.wait()
        count[s + 1] = count[s] + count_in[s]
    token_total = float(rows * fsdp_size * seq_size)
    scale = token_total / jnp.maximum(count[len(count_to)][:1], 1.0)
    weight[...] = down_rows(flags[...], rows) * scale[:, :1]

    @pl.loop(0, kv_heads)
    def _(j):
        on_hop(0, 2, j)

    first_hops(1)

    def blocks_of(m, part, j):
        return jnp.concatenate(
            [window[m, o, j, part * rows : (part + 1) * rows] for o in range(hops + 1)], axis=0
        )

    def columns(j):
        return pl.ds(pl.multiple_of(j * wide, wide), wide)

    def backward(j):
        k_win = blocks_of(0, 0, j)
        v_win = blocks_of(0, 1, j)
        q_all = stack_heads(q_prev[:, columns(j)])
        up_all = stack_heads(upstream[:, columns(j)]).astype(jnp.float32)
        d_all = (up_all * jnp.concatenate([weight[...]] * group, axis=0)).astype(jnp.bfloat16)
        expo, total = weights_t(k_win, q_all, bias[0], group)
        probs = expo * (1.0 / total)
        d_probs = dot_nt(v_win, d_all)
        delta = jnp.sum(probs * d_probs, axis=0, keepdims=True)
        d_scores = (probs * (d_probs - delta) * (HEAD_DIM ** (-0.5))).astype(jnp.bfloat16)
        dv = dot_nn(probs.astype(jnp.bfloat16), d_all).astype(jnp.bfloat16)
        dk = dot_nn(d_scores, q_all).astype(jnp.bfloat16)
        for o in range(hops + 1):
            grads[o, j, :rows] = dk[o * rows : (o + 1) * rows]
            grads[o, j, rows:] = dv[o * rows : (o + 1) * rows]
        dq_t = dot_nn(k_win.T, d_scores)
        dq_out[:, columns(j)] = jnp.concatenate(
            [dq_t[:, g * rows : (g + 1) * rows].T for g in range(group)], axis=1
        ).astype(dq_out.dtype)

    def forward(j):
        k_win = blocks_of(1, 0, j)
        v_win = blocks_of(1, 1, j)
        q_all = stack_heads(q_next[:, columns(j)])
        expo, total = weights_t(k_win, q_all, bias[1], group)
        out_t = dot_nn(v_win.T, expo.astype(jnp.bfloat16)) * (1.0 / total)
        attn_out[:, columns(j)] = jnp.concatenate(
            [out_t[:, g * rows : (g + 1) * rows].T for g in range(group)], axis=1
        ).astype(attn_out.dtype)

    def later_hops(m, j):
        for o in range(4, top + 1, 2):
            on_hop(m, o, j)

    def grad_swap(o, j):
        return pltpu.make_async_remote_copy(
            src_ref=grads.at[o, j],
            dst_ref=grad_in.at[o // 2, j],
            send_sem=grad_send.at[o, j],
            recv_sem=grad_recv.at[o, j],
            device_id=(row_of, partner),
            device_id_type=MESH,
        )

    def sum_back(o, j):
        return pltpu.make_async_remote_copy(
            src_ref=sums.at[o // 2 - 1, j],
            dst_ref=sums_in.at[o // 2 - 1, j],
            send_sem=grad_send.at[o, j],
            recv_sem=grad_recv.at[o, j],
            device_id=(row_of, me - 2),
            device_id_type=MESH,
        )

    def joined(o, j):
        even = jnp.where(parity == 0, 1.0, 0.0)
        acc = jnp.zeros(grads.shape[2:], jnp.float32)
        if o <= hops:
            acc = grads[o, j].astype(jnp.float32)
        if o + 1 <= hops:
            acc = acc + grad_in[o // 2, j].astype(jnp.float32) * even
        if o > 0:
            acc = acc + grad_in[o // 2 - 1, j].astype(jnp.float32) * (1.0 - even)
        if o + 2 <= top:
            acc = acc + sums_in[o // 2, j].astype(jnp.float32)
        return acc

    def send_sum(o, j):
        sums[o // 2 - 1, j] = joined(o, j).astype(sums.dtype)

        @pl.when(has_before)
        def _():
            sum_back(o, j).start()

    def arrive_sum(o, j):
        @pl.when(has_after)
        def _():
            sum_back(o, j).wait_recv()

    def first_sum(j):
        for o in range(1, hops + 1, 2):
            grad_swap(o, j).wait_recv()
        send_sum(top, j)

    def ready(m, j):
        for o in range(1, hops + 1, 2):
            arrive_swap(m, o, j)

    for copy in wide_copies:
        copy.wait()
    later_hops(0, 0)

    @pl.loop(0, kv_heads)
    def _(j):
        @pl.when(j + 1 < kv_heads)
        def _():
            later_hops(0, j + 1)

        ready(0, j)
        backward(j)
        for o in range(1, hops + 1, 2):
            grad_swap(o, j).start()

        @pl.when(j > 0)
        def _():
            first_sum(j - 1)

    first_sum(kv_heads - 1)

    @pl.loop(0, kv_heads)
    def _(j):
        on_hop(1, 2, j)
        for o in range(top - 2, 0, -2):
            arrive_sum(o + 2, j)
            send_sum(o, j)

    later_hops(1, 0)

    @pl.loop(0, kv_heads)
    def _(j):
        @pl.when(j + 1 < kv_heads)
        def _():
            later_hops(1, j + 1)

        arrive_sum(2, j)
        acc = joined(0, j).astype(jnp.bfloat16)
        spot = pl.ds(pl.multiple_of(j * HEAD_DIM, HEAD_DIM), HEAD_DIM)
        dk_out[:, spot] = acc[:rows]
        dv_out[:, spot] = acc[rows:]
        ready(1, j)
        forward(j)

    @pl.loop(0, kv_heads)
    def _(j):
        for m in range(2):
            for o in range(2, top + 1, 2):

                @pl.when(has_after & (me >= o - 2))
                def _(m=m, o=o):
                    hop(m, o, j).wait_send()

            for o in range(1, hops + 1, 2):

                @pl.when(partner >= o)
                def _(m=m, o=o):
                    swap(m, o, j).wait_send()

        for o in range(1, hops + 1, 2):
            grad_swap(o, j).wait_send()
        for o in range(2, top + 1, 2):

            @pl.when(has_before)
            def _(o=o):
                sum_back(o, j).wait_send()


def place_kernel(*refs):
    half = len(refs) // 2
    for source, target in zip(refs[:half], refs[half:]):
        target[...] = source[...]


def placed(parts, arrays):
    steps = math.gcd(parts, 4)
    specs = [
        pl.BlockSpec((a.shape[0], a.shape[1] // steps), lambda j: (0, j)) for a in arrays
    ]
    return tuple(
        pl.pallas_call(
            place_kernel,
            grid=(steps,),
            in_specs=specs,
            out_specs=specs,
            out_shape=[jax.ShapeDtypeStruct(a.shape, a.dtype) for a in arrays],
            name="place",
        )(*arrays)
    )


def make_body(fsdp_size, seq_size):
    def body(q_next, k_next, v_next, seg_next, q_prev, k_prev, v_prev, seg_prev, upstream, flags):
        rows, width = k_next.shape
        kv_heads = width // HEAD_DIM
        hops = min((min(SEG_MOST, rows * seq_size) - 2) // rows + 1, seq_size - 1)
        top = hops + hops % 2
        steps = fsdp_size.bit_length() + seq_size.bit_length() - 2
        piece = (2 * rows, HEAD_DIM)
        near = pl.BlockSpec(memory_space=pltpu.VMEM)
        far = pl.BlockSpec(memory_space=pl.ANY)
        call = pl.pallas_call(
            functools.partial(kernel, hops, (fsdp_size, seq_size)),
            in_specs=[far, far, far, near, far, far, far, near, far, near],
            out_specs=[near] * 4,
            out_shape=[
                jax.ShapeDtypeStruct(q_next.shape, jnp.bfloat16),
                jax.ShapeDtypeStruct(q_prev.shape, jnp.bfloat16),
                jax.ShapeDtypeStruct(k_prev.shape, jnp.bfloat16),
                jax.ShapeDtypeStruct(v_prev.shape, jnp.bfloat16),
            ],
            scratch_shapes=[
                pltpu.VMEM(q_next.shape, jnp.bfloat16),
                pltpu.VMEM(q_prev.shape, jnp.bfloat16),
                pltpu.VMEM(upstream.shape, jnp.bfloat16),
                pltpu.SemaphoreType.DMA((3,)),
                pltpu.VMEM((2, top + 1, kv_heads) + piece, jnp.bfloat16),
                pltpu.VMEM((2, (hops + 1) * rows, rows), jnp.float32),
                pltpu.VMEM((rows, rows), jnp.float32),
                pltpu.VMEM((hops + 1, kv_heads) + piece, jnp.bfloat16),
                pltpu.VMEM(((hops + 1) // 2, kv_heads) + piece, jnp.bfloat16),
                pltpu.VMEM((top // 2, kv_heads) + piece, jnp.bfloat16),
                pltpu.VMEM((top // 2, kv_heads) + piece, jnp.bfloat16),
                pltpu.VMEM((steps + 1, 8, 128), jnp.float32),
                pltpu.VMEM((steps, 8, 128), jnp.float32),
                pltpu.SemaphoreType.DMA((2, 2, kv_heads)),
                pltpu.SemaphoreType.DMA((2, top + 1, kv_heads)),
                pltpu.SemaphoreType.DMA((2, top + 1, kv_heads)),
                pltpu.SemaphoreType.DMA((top + 1, kv_heads)),
                pltpu.SemaphoreType.DMA((top + 1, kv_heads)),
                pltpu.SemaphoreType.DMA((steps,)),
                pltpu.SemaphoreType.DMA((steps,)),
            ],
            compiler_params=pltpu.CompilerParams(
                collective_id=0, has_side_effects=True, vmem_limit_bytes=60 * 1024 * 1024
            ),
            name="attention_pair",
        )
        return placed(
            kv_heads,
            call(
                q_next,
                k_next,
                v_next,
                seg_next,
                q_prev,
                k_prev,
                v_prev,
                seg_prev,
                upstream,
                flags,
            ),
        )

    return body


def solution(mesh):
    tokens = P(("fsdp", "seq"), None)
    ids = P("fsdp", None)
    return jax.shard_map(
        make_body(mesh.shape["fsdp"], mesh.shape["seq"]),
        mesh=mesh,
        in_specs=(
            tokens,
            tokens,
            tokens,
            ids,
            tokens,
            tokens,
            tokens,
            ids,
            tokens,
            P("fsdp", "seq"),
        ),
        out_specs=(tokens, tokens, tokens, tokens),
        check_vma=False,
    )
```
